32 devices in a mesh: seq: 2 (over x), fsdp: 16 (over z, y, core).
Axes of the slice: x: 2, y: 2, z: 4, core: 2. Of those that a mesh axis runs over, the one named last changes fastest.
Arguments:
- frames_in: float32 [16, 256, 768], P('fsdp', 'seq'), may hold values from -6 to 6
- cotangent: float32 [16, 256, 768], P('fsdp', 'seq'), may hold values from -6 to 6
- first_gain: bfloat16 [1, 768], P(None, 'fsdp'), may hold values from 0.099609375 to 1.8984375
- first_bias: bfloat16 [1, 768], P(None, 'fsdp'), may hold values from -3 to 3
- query_weight: bfloat16 [1, 768, 768], P(None, 'fsdp'), may hold values from -0.21875 to 0.21875
- query_bias: bfloat16 [1, 768], P(None, 'fsdp'), may hold values from -3 to 3
- key_weight: bfloat16 [1, 768, 768], P(None, 'fsdp'), may hold values from -0.21875 to 0.21875
- value_weight: bfloat16 [1, 768, 768], P(None, 'fsdp'), may hold values from -0.21875 to 0.21875
- value_bias: bfloat16 [1, 768], P(None, 'fsdp'), may hold values from -3 to 3
- out_weight: bfloat16 [1, 768, 768], P(None, 'fsdp'), may hold values from -3.5 to 3.5
- out_bias: bfloat16 [1, 768], P(None, 'fsdp'), may hold values from -3 to 3
- second_gain: bfloat16 [1, 768], P(None, 'fsdp'), may hold values from 0.099609375 to 1.8984375
- second_bias: bfloat16 [1, 768], P(None, 'fsdp'), may hold values from -3 to 3
- up_weight: bfloat16 [1, 768, 3072], P(None, 'fsdp'), may hold values from -0.21875 to 0.21875
- up_bias: bfloat16 [1, 3072], P(None, 'fsdp'), may hold values from -3 to 3
- down_weight: bfloat16 [1, 3072, 768], P(None, 'fsdp'), may hold values from -0.109375 to 0.109375
- down_bias: bfloat16 [1, 768], P(None, 'fsdp'), may hold values from -3 to 3
Outputs:
- outputs: float32 [16, 256, 768], P('fsdp', 'seq')
- input_gradient: float32 [16, 256, 768], P('fsdp', 'seq')
- first_gain_gradient: float32 [1, 768], P(None, 'fsdp')
- first_bias_gradient: float32 [1, 768], P(None, 'fsdp')
- query_weight_gradient: float32 [1, 768, 768], P(None, 'fsdp')
- query_bias_gradient: float32 [1, 768], P(None, 'fsdp')
- key_weight_gradient: float32 [1, 768, 768], P(None, 'fsdp')
- value_weight_gradient: float32 [1, 768, 768], P(None, 'fsdp')
- value_bias_gradient: float32 [1, 768], P(None, 'fsdp')
- out_weight_gradient: float32 [1, 768, 768], P(None, 'fsdp')
- out_bias_gradient: float32 [1, 768], P(None, 'fsdp')
- second_gain_gradient: float32 [1, 768], P(None, 'fsdp')
- second_bias_gradient: float32 [1, 768], P(None, 'fsdp')
- up_weight_gradient: float32 [1, 768, 3072], P(None, 'fsdp')
- up_bias_gradient: float32 [1, 3072], P(None, 'fsdp')
- down_weight_gradient: float32 [1, 3072, 768], P(None, 'fsdp')
- down_bias_gradient: float32 [1, 768], P(None, 'fsdp')
The draws below stay inside these ranges and needn't reach their ends.
All inputs are finite; a program needn't handle non-finite values.
Results may differ from the reference program's by a relative error of at most 0.012.
The reference program's roundings to bfloat16 on the way count: a program that leaves them out, or rounds other values in their place, can miss the bound.
Values may be sent and summed in bfloat16 or wider, within the bound.
A program may use at most 128 MiB of HBM per device.

```python
import jax
import jax.numpy as jnp
from jax import lax

D = 768
HEAD_DIM = 64
FF = 3072
LAYERS = 1
FRAMES = 256
CLIPS = 16


def strengthened(array, key, source, target, shards_of, factor):
    owner, partner = [(jnp.arange(array.shape[position]) // (array.shape[position] // shards_of)).reshape([-1 if axis == position else 1 for axis in range(array.ndim)]) for position in (source, target)]
    chosen = jax.random.permutation(key, shards_of)[partner]
    strong = (owner == chosen) | (owner == (partner + shards_of // 2) % shards_of)
    return jnp.where(strong, factor * array, array)


def block_levels(own_key, extent, pieces, least, largest):
    def one(axis_at, blocks):
        heights = jax.random.uniform(jax.random.fold_in(jax.random.fold_in(own_key, 6), axis_at), (blocks,), jnp.float32, least / len(pieces), largest / len(pieces))
        return jnp.repeat(jnp.exp(heights), extent[axis_at] // blocks).reshape((-1,) + (1,) * (len(extent) - axis_at - 1))

    level = one(*pieces[0])
    for cut in pieces[1:]:
        level = level * one(*cut)
    return level


def normal_values(key, dims, width, most, cuts=(), kind=jnp.bfloat16):
    factor_of = block_levels(key, dims, cuts, -0.22, 0.18) if cuts else 1.0
    drawn = jax.random.normal(key, dims, jnp.float32) * width * factor_of
    return jnp.minimum(jnp.maximum(drawn, -most), most).astype(kind)


def heavy_noise(key, extent, scale, limit, split, heavy, kind=jnp.bfloat16):
    array = scale * jax.random.normal(key, extent, jnp.float32)
    if split:
        array = array * block_levels(key, extent, split, -0.22, 0.18)
    return jnp.clip(strengthened(array, jax.random.fold_in(key, 3), *heavy), -limit, limit).astype(kind)


def setup_inputs(seed: int = 0) -> dict:
    splits = jax.random.split(jax.random.key(seed), 18)
    return {
        "frames_in": normal_values(splits[0], (CLIPS, FRAMES, D), 1.0, 6.0, ((0, 16), (1, 2)), jnp.float32),
        "cotangent": heavy_noise(splits[1], (CLIPS, FRAMES, D), 1.0, 6.0, ((0, 16), (1, 2)), (0, 2, 16, 2.0), jnp.float32),
        "first_gain": jnp.clip(1.0 + 0.18 * jax.random.normal(splits[2], (LAYERS, D), jnp.float32), 0.099609375, 1.8984375).astype(jnp.bfloat16),
        "first_bias": normal_values(splits[3], (LAYERS, D), 0.5, 3.0, ((1, 16),)),
        "query_weight": normal_values(splits[4], (LAYERS, D, D), D ** -0.5, 0.21875, ((1, 16),)),
        "query_bias": normal_values(splits[5], (LAYERS, D), 0.5, 3.0, ((1, 16),)),
        "key_weight": normal_values(splits[6], (LAYERS, D, D), D ** -0.5, 0.21875, ((1, 16),)),
        "value_weight": normal_values(splits[7], (LAYERS, D, D), D ** -0.5, 0.21875, ((1, 16),)),
        "value_bias": normal_values(splits[8], (LAYERS, D), 0.5, 3.0, ((1, 16),)),
        "out_weight": normal_values(splits[9], (LAYERS, D, D), (max(1, D // FRAMES)) ** -0.5, 3.5, ((1, 16),)),
        "out_bias": normal_values(splits[10], (LAYERS, D), 0.5, 3.0, ((1, 16),)),
        "second_gain": jnp.clip(1.0 + 0.18 * jax.random.normal(splits[11], (LAYERS, D), jnp.float32), 0.099609375, 1.8984375).astype(jnp.bfloat16),
        "second_bias": normal_values(splits[12], (LAYERS, D), 0.5, 3.0, ((1, 16),)),
        "up_weight": normal_values(splits[13], (LAYERS, D, FF), D ** -0.5, 0.21875, ((1, 16),)),
        "up_bias": normal_values(splits[14], (LAYERS, FF), 0.5, 3.0, ((1, 16),)),
        "down_weight": normal_values(splits[15], (LAYERS, FF, D), FF ** -0.5, 0.109375, ((1, 16),)),
        "down_bias": normal_values(splits[16], (LAYERS, D), 0.5, 3.0, ((1, 16),)),
    }


EPSILON = 1e-05
ROOT_HALF = 0.7071067811865476
INV_ROOT_TAU = 0.3989422804014327

def matmul(left, right):
    return jnp.dot(left, right, preferred_element_type=jnp.float32)

def contract_rows(left, right):
    return lax.dot_general(left, right, (((0,), (0,)), ((), ())), preferred_element_type=jnp.float32)

def contract_cols(left, right):
    return lax.dot_general(left, right, (((1,), (1,)), ((), ())), preferred_element_type=jnp.float32)

def round_low(values):
    return lax.optimization_barrier(values.astype(jnp.bfloat16))

def layer_norm(residual, gain, offset):
    centre = residual - lax.optimization_barrier(jnp.mean(residual, axis=-1, keepdims=True))
    inv_std = lax.rsqrt(lax.optimization_barrier(jnp.mean(centre * centre, axis=-1, keepdims=True)) + EPSILON)
    normed = centre * inv_std
    return (normed * gain.astype(jnp.float32) + offset.astype(jnp.float32), normed, inv_std)

def norm_grad(upstream, normed, inv_std, gain):
    scaled = upstream * gain.astype(jnp.float32)
    spread = scaled - lax.optimization_barrier(jnp.mean(scaled, axis=-1, keepdims=True))
    return (spread - normed * lax.optimization_barrier(jnp.mean(scaled * normed, axis=-1, keepdims=True))) * inv_std

def gelu_exact(pre_act):
    return 0.5 * pre_act * (1.0 + lax.erf(pre_act * ROOT_HALF))

def gelu_slope(pre_act):
    return 0.5 * (1.0 + lax.erf(pre_act * ROOT_HALF)) + pre_act * jnp.exp(-0.5 * pre_act * pre_act) * INV_ROOT_TAU

def split_heads(rows):
    return rows.astype(jnp.float32).reshape(rows.shape[0], rows.shape[1] // HEAD_DIM, HEAD_DIM)

def attend(query_rows, key_rows, value_rows):
    score_scale = HEAD_DIM ** (-0.5)
    query_heads = split_heads(query_rows)
    key_heads = split_heads(key_rows)
    value_heads = split_heads(value_rows)
    scores = jnp.einsum('qhd,khd->hqk', query_heads, key_heads) * score_scale
    row_top = lax.optimization_barrier(jnp.max(scores, axis=-1, keepdims=True))
    log_total = row_top + jnp.log(lax.optimization_barrier(jnp.sum(jnp.exp(scores - row_top), axis=-1, keepdims=True)))
    weights_low = round_low(jnp.exp(scores - log_total))
    context = jnp.einsum('hqk,khd->qhd', weights_low.astype(jnp.float32), value_heads)
    return (round_low(context.reshape(query_rows.shape)), log_total)

def attend_back(query_rows, key_rows, value_rows, log_total, context_gradient):
    score_scale = HEAD_DIM ** (-0.5)
    row_shape = query_rows.shape
    query_heads = split_heads(query_rows)
    key_heads = split_heads(key_rows)
    value_heads = split_heads(value_rows)
    gradient_heads = split_heads(context_gradient)
    scores = jnp.einsum('qhd,khd->hqk', query_heads, key_heads) * score_scale
    weights = jnp.exp(scores - log_total)
    weights_low = round_low(weights)
    value_gradient = jnp.einsum('hqk,qhd->khd', weights_low.astype(jnp.float32), gradient_heads)
    prob_gradient = jnp.einsum('qhd,khd->hqk', gradient_heads, value_heads)
    score_gradient = round_low(weights * (prob_gradient - lax.optimization_barrier(jnp.sum(weights * prob_gradient, axis=-1, keepdims=True))) * score_scale)
    score_wide = score_gradient.astype(jnp.float32)
    query_gradient = jnp.einsum('hqk,khd->qhd', score_wide, key_heads)
    key_gradient = jnp.einsum('hqk,qhd->khd', score_wide, query_heads)
    return (round_low(query_gradient.reshape(row_shape)), round_low(key_gradient.reshape(row_shape)), round_low(value_gradient.reshape(row_shape)))

def forward_layer(residual, params):
    hidden_wide, normed_in, inv_in = layer_norm(residual, params[0], params[1])
    hidden = round_low(hidden_wide)
    query_rows = round_low(matmul(hidden, params[2]) + params[3].astype(jnp.float32))
    key_rows = round_low(matmul(hidden, params[4]))
    value_rows = round_low(matmul(hidden, params[5]) + params[6].astype(jnp.float32))
    context, log_total = attend(query_rows, key_rows, value_rows)
    middle = residual + matmul(context, params[7]) + params[8].astype(jnp.float32)
    mid_wide, normed_mid, inv_mid = layer_norm(middle, params[9], params[10])
    hidden_mid = round_low(mid_wide)
    pre_act = matmul(hidden_mid, params[11]) + params[12].astype(jnp.float32)
    activated = round_low(gelu_exact(pre_act))
    result = middle + matmul(activated, params[13]) + params[14].astype(jnp.float32)
    return (result, (hidden, normed_in, inv_in, query_rows, key_rows, value_rows, log_total, context, normed_mid, inv_mid, hidden_mid, pre_act, activated))

def backward_layer(upstream, stored, params):
    hidden, normed_in, inv_in, query_rows, key_rows, value_rows, log_total, context, normed_mid, inv_mid, hidden_mid, pre_act, activated = stored
    upstream_low = round_low(upstream)
    down_weight_gradient = contract_rows(activated, upstream_low)
    down_bias_gradient = lax.optimization_barrier(jnp.sum(upstream, axis=0))
    pre_gradient = contract_cols(upstream_low, params[13]) * gelu_slope(pre_act)
    pre_low = round_low(pre_gradient)
    up_weight_gradient = contract_rows(hidden_mid, pre_low)
    up_bias_gradient = lax.optimization_barrier(jnp.sum(pre_gradient, axis=0))
    mid_hidden_gradient = contract_cols(pre_low, params[11])
    second_gain_gradient = lax.optimization_barrier(jnp.sum(mid_hidden_gradient * normed_mid, axis=0))
    second_bias_gradient = lax.optimization_barrier(jnp.sum(mid_hidden_gradient, axis=0))
    middle_gradient = upstream + norm_grad(mid_hidden_gradient, normed_mid, inv_mid, params[9])
    middle_low = round_low(middle_gradient)
    out_weight_gradient = contract_rows(context, middle_low)
    out_bias_gradient = lax.optimization_barrier(jnp.sum(middle_gradient, axis=0))
    context_gradient = round_low(contract_cols(middle_low, params[7]))
    query_gradient, key_gradient, value_gradient = attend_back(query_rows, key_rows, value_rows, log_total, context_gradient)
    query_weight_gradient = contract_rows(hidden, query_gradient)
    query_bias_gradient = lax.optimization_barrier(jnp.sum(query_gradient.astype(jnp.float32), axis=0))
    key_weight_gradient = contract_rows(hidden, key_gradient)
    value_weight_gradient = contract_rows(hidden, value_gradient)
    value_bias_gradient = lax.optimization_barrier(jnp.sum(value_gradient.astype(jnp.float32), axis=0))
    hidden_gradient = contract_cols(query_gradient, params[2]) + contract_cols(key_gradient, params[4]) + contract_cols(value_gradient, params[5])
    first_gain_gradient = lax.optimization_barrier(jnp.sum(hidden_gradient * normed_in, axis=0))
    first_bias_gradient = lax.optimization_barrier(jnp.sum(hidden_gradient, axis=0))
    input_gradient = middle_gradient + norm_grad(hidden_gradient, normed_in, inv_in, params[0])
    return (input_gradient, (first_gain_gradient, first_bias_gradient, query_weight_gradient, query_bias_gradient, key_weight_gradient, value_weight_gradient, value_bias_gradient, out_weight_gradient, out_bias_gradient, second_gain_gradient, second_bias_gradient, up_weight_gradient, up_bias_gradient, down_weight_gradient, down_bias_gradient))

def reference(frames_in, cotangent, first_gain, first_bias, query_weight, query_bias, key_weight, value_weight, value_bias, out_weight, out_bias, second_gain, second_bias, up_weight, up_bias, down_weight, down_bias):
    stacks = (first_gain, first_bias, query_weight, query_bias, key_weight, value_weight, value_bias, out_weight, out_bias, second_gain, second_bias, up_weight, up_bias, down_weight, down_bias)

    def per_clip(totals, clip_pair):
        residual, upstream = clip_pair
        stored_all = []
        for layer_num in range(LAYERS):
            params = tuple((stack[layer_num] for stack in stacks))
            residual, stored = forward_layer(residual, params)
            stored_all.append(stored)
        layer_grads = [None] * LAYERS
        for layer_num in reversed(range(LAYERS)):
            params = tuple((stack[layer_num] for stack in stacks))
            upstream, gradients = backward_layer(upstream, stored_all[layer_num], params)
            layer_grads[layer_num] = gradients
        summed = tuple((totals[member] + jnp.stack([layer_grads[layer_num][member] for layer_num in range(LAYERS)]) for member in range(len(stacks))))
        return (summed, (residual, upstream))
    zeros = tuple((jnp.zeros(stack.shape, jnp.float32) for stack in stacks))
    totals, finals = lax.scan(per_clip, zeros, (frames_in, cotangent))
    return (finals[0], finals[1], totals[0], totals[1], totals[2], totals[3], totals[4], totals[5], totals[6], totals[7], totals[8], totals[9], totals[10], totals[11], totals[12], totals[13], totals[14])
```

```python
import jax
import jax.numpy as jnp
from jax import lax
from jax.sharding import PartitionSpec as P

HEAD_DIM = 64


EPSILON = 1e-05
ROOT_HALF = 0.7071067811865476
INV_ROOT_TAU = 0.3989422804014327


def matmul(left, right):
    return jnp.dot(left, right, preferred_element_type=jnp.float32)


def contract_rows(left, right):
    return lax.dot_general(
        left, right, (((0,), (0,)), ((), ())), preferred_element_type=jnp.float32
    )


def contract_cols(left, right):
    return lax.dot_general(
        left, right, (((1,), (1,)), ((), ())), preferred_element_type=jnp.float32
    )


def layer_norm(residual, gain, offset):
    centre = residual - jnp.mean(residual, axis=-1, keepdims=True)
    inv_std = lax.rsqrt(jnp.mean(centre * centre, axis=-1, keepdims=True) + EPSILON)
    normed = centre * inv_std
    return (normed * gain.astype(jnp.float32) + offset.astype(jnp.float32), normed, inv_std)


def norm_grad(upstream, normed, inv_std, gain):
    scaled = upstream * gain.astype(jnp.float32)
    spread = scaled - jnp.mean(scaled, axis=-1, keepdims=True)
    return (spread - normed * jnp.mean(scaled * normed, axis=-1, keepdims=True)) * inv_std


def gelu_exact(pre_act):
    return 0.5 * pre_act * (1.0 + lax.erf(pre_act * ROOT_HALF))


def gelu_slope(pre_act):
    return (
        0.5 * (1.0 + lax.erf(pre_act * ROOT_HALF))
        + pre_act * jnp.exp(-0.5 * pre_act * pre_act) * INV_ROOT_TAU
    )


def split_heads(rows):
    return rows.reshape(rows.shape[0], rows.shape[1] // HEAD_DIM, HEAD_DIM)


def attend(query_rows, key_rows, value_rows):
    score_scale = HEAD_DIM ** (-0.5)
    query_heads = split_heads(query_rows)
    key_heads = split_heads(key_rows)
    value_heads = split_heads(value_rows)
    scores = (
        jnp.einsum("qhd,khd->hqk", query_heads, key_heads, preferred_element_type=jnp.float32)
        * score_scale
    )
    row_top = jnp.max(scores, axis=-1, keepdims=True)
    log_total = row_top + jnp.log(jnp.sum(jnp.exp(scores - row_top), axis=-1, keepdims=True))
    weights = jnp.exp(scores - log_total)
    context = jnp.einsum(
        "hqk,khd->qhd",
        weights.astype(jnp.bfloat16),
        value_heads,
        preferred_element_type=jnp.float32,
    )
    return (context.reshape(query_rows.shape).astype(jnp.bfloat16), weights)


def attend_back(query_rows, key_rows, value_rows, weights, context_gradient):
    score_scale = HEAD_DIM ** (-0.5)
    row_shape = query_rows.shape
    query_heads = split_heads(query_rows)
    key_heads = split_heads(key_rows)
    value_heads = split_heads(value_rows)
    gradient_heads = split_heads(context_gradient)
    value_gradient = jnp.einsum(
        "hqk,qhd->khd",
        weights.astype(jnp.bfloat16),
        gradient_heads,
        preferred_element_type=jnp.float32,
    )
    prob_gradient = jnp.einsum(
        "qhd,khd->hqk", gradient_heads, value_heads, preferred_element_type=jnp.float32
    )
    score_gradient = (
        weights
        * (prob_gradient - jnp.sum(weights * prob_gradient, axis=-1, keepdims=True))
        * score_scale
    ).astype(jnp.bfloat16)
    query_gradient = jnp.einsum(
        "hqk,khd->qhd", score_gradient, key_heads, preferred_element_type=jnp.float32
    )
    key_gradient = jnp.einsum(
        "hqk,qhd->khd", score_gradient, query_heads, preferred_element_type=jnp.float32
    )
    return tuple(
        part.reshape(row_shape).astype(jnp.bfloat16)
        for part in (query_gradient, key_gradient, value_gradient)
    )


VECTORS = (0, 1, 3, 6, 8, 9, 10, 12, 14)
MATRICES = (2, 4, 5, 7, 11, 13)
PAD_ROWS = 16


def cut_columns(rows, width):
    blocks = rows.shape[-1] // width
    if blocks == 1:
        return rows
    return jnp.concatenate(
        [rows[..., i * width : (i + 1) * width] for i in range(blocks)], axis=-2
    )


def join_columns(rows, blocks):
    if blocks == 1:
        return rows
    size = rows.shape[-2] // blocks
    return jnp.concatenate(
        [rows[..., i * size : (i + 1) * size, :] for i in range(blocks)], axis=-1
    )


def gather_layer(shards, width):
    pieces = [cut_columns(shards[i], width) for i in MATRICES]
    vector = jnp.concatenate([shards[i] for i in VECTORS])
    vector = jnp.pad(vector, (0, PAD_ROWS * width - vector.shape[0]))
    pieces.append(vector.reshape(PAD_ROWS, width))
    packed = lax.all_gather(jnp.concatenate(pieces, axis=0), "fsdp", axis=0, tiled=False)
    params = [None] * len(shards)
    start = 0
    for i in MATRICES:
        blocks = shards[i].shape[1] // width
        size = shards[i].shape[0] * blocks
        part = join_columns(packed[:, start : start + size], blocks)
        params[i] = part.reshape(-1, shards[i].shape[1])
        start += size
    vectors = packed[:, start:].reshape(packed.shape[0], -1)
    start = 0
    for i in VECTORS:
        size = shards[i].shape[0]
        params[i] = vectors[:, start : start + size].reshape(-1)
        start += size
    return params


def reduce_gradients(gradients, shards, width, seq_size, seq_index, fsdp_size):
    part_width = width // seq_size
    pieces = []
    for i in MATRICES:
        blocks = shards[i].shape[1] // width
        rows = gradients[i].astype(jnp.bfloat16)
        rows = rows.reshape(fsdp_size, shards[i].shape[0], rows.shape[1])
        pieces.append(cut_columns(rows, part_width))
    vector = jnp.concatenate(
        [gradients[i].reshape(fsdp_size, -1) for i in VECTORS], axis=1
    ).astype(jnp.bfloat16)
    vector = jnp.pad(vector, ((0, 0), (0, PAD_ROWS * width - vector.shape[1])))
    vector = vector.reshape(fsdp_size, PAD_ROWS * seq_size, part_width)
    pieces.append(lax.dynamic_slice_in_dim(vector, seq_index * PAD_ROWS, PAD_ROWS, axis=1))
    packed = jnp.concatenate(pieces, axis=1)
    mine = lax.psum_scatter(packed, "fsdp", scatter_dimension=0, tiled=False)
    both = lax.all_gather(mine, "seq", axis=0, tiled=False)
    reduced = [None] * len(shards)
    start = 0
    for i in MATRICES:
        blocks = shards[i].shape[1] // width
        size = shards[i].shape[0] * blocks
        part = join_columns(both[:, start : start + size], blocks)
        whole = jnp.concatenate([part[s] for s in range(seq_size)], axis=-1)
        reduced[i] = whole.astype(jnp.float32)[None]
        start += size
    vector = both[:, start:].reshape(-1).astype(jnp.float32)
    start = 0
    for i in VECTORS:
        size = shards[i].shape[0]
        reduced[i] = vector[start : start + size][None]
        start += size
    return reduced


def on_device(frames_in, cotangent, *stacks):
    width = frames_in.shape[2]
    seq_size = lax.axis_size("seq")
    seq_index = lax.axis_index("seq")
    fsdp_size = lax.axis_size("fsdp")
    shards = [stack[0] for stack in stacks]
    own = frames_in.shape[1]

    mine = jnp.stack([frames_in[0], cotangent[0]])
    if seq_size == 2:
        other = lax.ppermute(mine, "seq", [(0, 1), (1, 0)])
        first = seq_index == 0
        rows = jnp.concatenate(
            [jnp.where(first, mine, other), jnp.where(first, other, mine)], axis=1
        )
    else:
        rows = lax.all_gather(mine, "seq", axis=1, tiled=True)
    residual, upstream = rows[0], rows[1]
    params = gather_layer(shards, width)

    def own_columns(matrix):
        size = matrix.shape[1] // seq_size
        return lax.dynamic_slice_in_dim(matrix, seq_index * size, size, axis=1)

    def own_rows(matrix):
        return lax.dynamic_slice_in_dim(matrix, seq_index * own, own, axis=0)[None]

    wide = [None if i in MATRICES else p.astype(jnp.float32) for i, p in enumerate(params)]

    hidden_wide, normed_in, inv_in = layer_norm(residual, params[0], params[1])
    hidden = hidden_wide.astype(jnp.bfloat16)
    query_rows = (matmul(hidden, params[2]) + wide[3]).astype(jnp.bfloat16)
    key_rows = matmul(hidden, params[4]).astype(jnp.bfloat16)
    value_rows = (matmul(hidden, params[5]) + wide[6]).astype(jnp.bfloat16)
    context, weights = attend(query_rows, key_rows, value_rows)
    middle = residual + matmul(context, params[7]) + wide[8]
    mid_wide, normed_mid, inv_mid = layer_norm(middle, params[9], params[10])
    hidden_mid = mid_wide.astype(jnp.bfloat16)
    pre_act = matmul(hidden_mid, params[11]) + wide[12]
    activated = gelu_exact(pre_act).astype(jnp.bfloat16)
    own_activated = own_rows(activated)[0]
    outputs = own_rows(middle)[0] + matmul(own_activated, params[13]) + wide[14]

    gradients = [None] * len(stacks)
    upstream_low = upstream.astype(jnp.bfloat16)
    gradients[13] = contract_rows(activated, own_columns(upstream_low))
    gradients[14] = jnp.sum(upstream, axis=0)
    pre_gradient = contract_cols(upstream_low, params[13]) * gelu_slope(pre_act)
    pre_low = pre_gradient.astype(jnp.bfloat16)
    gradients[11] = contract_rows(hidden_mid, own_columns(pre_low))
    gradients[12] = jnp.sum(pre_gradient, axis=0)
    mid_hidden_gradient = contract_cols(pre_low, params[11])
    gradients[9] = jnp.sum(mid_hidden_gradient * normed_mid, axis=0)
    gradients[10] = jnp.sum(mid_hidden_gradient, axis=0)
    middle_gradient = upstream + norm_grad(mid_hidden_gradient, normed_mid, inv_mid, params[9])
    middle_low = middle_gradient.astype(jnp.bfloat16)
    gradients[7] = contract_rows(context, own_columns(middle_low))
    gradients[8] = jnp.sum(middle_gradient, axis=0)
    context_gradient = contract_cols(middle_low, params[7]).astype(jnp.bfloat16)
    query_gradient, key_gradient, value_gradient = attend_back(
        query_rows, key_rows, value_rows, weights, context_gradient
    )
    gradients[2] = contract_rows(hidden, own_columns(query_gradient))
    gradients[3] = jnp.sum(query_gradient.astype(jnp.float32), axis=0)
    gradients[4] = contract_rows(hidden, own_columns(key_gradient))
    gradients[5] = contract_rows(hidden, own_columns(value_gradient))
    gradients[6] = jnp.sum(value_gradient.astype(jnp.float32), axis=0)
    hidden_gradient = (
        contract_cols(query_gradient, params[2])
        + contract_cols(key_gradient, params[4])
        + contract_cols(value_gradient, params[5])
    )
    gradients[0] = jnp.sum(hidden_gradient * normed_in, axis=0)
    gradients[1] = jnp.sum(hidden_gradient, axis=0)
    input_gradient = middle_gradient + norm_grad(hidden_gradient, normed_in, inv_in, params[0])
    reduced = reduce_gradients(gradients, shards, width, seq_size, seq_index, fsdp_size)
    return (outputs[None], own_rows(input_gradient), *reduced)


def solution(mesh):
    return jax.shard_map(
        on_device,
        mesh=mesh,
        in_specs=(
            P("fsdp", "seq", None),
            P("fsdp", "seq", None),
            P(None, "fsdp"),
            P(None, "fsdp"),
            P(None, "fsdp", None),
            P(None, "fsdp"),
            P(None, "fsdp", None),
            P(None, "fsdp", None),
            P(None, "fsdp"),
            P(None, "fsdp", None),
            P(None, "fsdp"),
            P(None, "fsdp"),
            P(None, "fsdp"),
            P(None, "fsdp", None),
            P(None, "fsdp"),
            P(None, "fsdp", None),
            P(None, "fsdp"),
        ),
        out_specs=(
            P("fsdp", "seq", None),
            P("fsdp", "seq", None),
            P(None, "fsdp"),
            P(None, "fsdp"),
            P(None, "fsdp", None),
            P(None, "fsdp"),
            P(None, "fsdp", None),
            P(None, "fsdp", None),
            P(None, "fsdp"),
            P(None, "fsdp", None),
            P(None, "fsdp"),
            P(None, "fsdp"),
            P(None, "fsdp"),
            P(None, "fsdp", None),
            P(None, "fsdp"),
            P(None, "fsdp", None),
            P(None, "fsdp"),
        ),
        check_vma=False,
    )
```
